32 devices in a mesh: slides: 2 (over y), seq: 16 (over z, x, core), mp: 1.
Axes of the slice: x: 2, y: 2, z: 4, core: 2. Of those that a mesh axis runs over, the one named last changes fastest.
Arguments:
- tokens: bfloat16 [32768, 768], P(('slides', 'seq', 'mp')), parts along dimension 0, may hold values from -6 to 6
- attn_gain: float32 [768], replicated, may hold values from 0.25 to 1.75
- query_first: bfloat16 [768, 768], P(None, 'mp'), may hold values from -4 to 4
- key_first: bfloat16 [768, 768], P(None, 'mp'), may hold values from -4 to 4
- segment_value: bfloat16 [768, 768], P(None, 'mp'), may hold values from -0.21875 to 0.21875
- output_first: bfloat16 [768, 768], P('mp'), may hold values from -0.875 to 0.875
- mlp_gain: float32 [768], replicated, may hold values from 0.25 to 1.75
- up_weight: bfloat16 [768, 3072], P(None, 'mp'), may hold values from -0.21875 to 0.21875
- down_weight: bfloat16 [3072, 768], P('mp'), may hold values from -0.109375 to 0.109375
- second_gain: float32 [768], replicated, may hold values from 0.25 to 1.75
- query_second: bfloat16 [768, 768], P(None, 'mp'), may hold values from -4 to 4
- key_second: bfloat16 [768, 768], P(None, 'mp'), may hold values from -4 to 4
- value_second: bfloat16 [768, 768], P(None, 'mp'), may hold values from -0.21875 to 0.21875
- output_second: bfloat16 [768, 768], P('mp'), may hold values from -0.875 to 0.875
- segment_offset: int32 [16], P('mp'), may hold values from 0 to 63
- global_offset: int32 [16], P('mp'), may hold values from 0 to 63
Outputs:
- encoded: bfloat16 [32768, 768], P(('slides', 'seq', 'mp')), parts along dimension 0
The draws below stay inside these ranges and needn't reach their ends.
There are 2 independent parts, one for each index of `slides`. The reference program is written for one: setup_inputs(seed, part) draws one part's arguments, and reference() takes and returns one part's arrays. A program takes and returns all parts, laid end to end along the dimension named above; an argument that names none is the same for every part. Nothing has to cross between parts.
All inputs are finite; a program needn't handle non-finite values.
Results may differ from the reference program's by a relative error of at most 0.03.
The reference program's roundings to bfloat16 on the way count: a program that leaves them out, or rounds other values in their place, can miss the bound.
Values may be sent and summed in bfloat16 or wider, within the bound.
A program may use at most 128 MiB of HBM per device.

```python
import math
import jax
import jax.numpy as jnp
from jax import lax

D = 768
HEADS = 16
FF = 3072
HEAD_DIM = 48
KEYS = 256
TOK_DEV = 1024
SEG_DEV = 16
TOKENS = 16384
N_SEQ = 16


def weight_pair(key, layer):
    base_key = jax.random.fold_in(key, 7100 + layer)
    first_key, whole_sequence_key = jax.random.split(base_key, 2)
    common = jax.random.truncated_normal(first_key, -4.0, 4.0, (D, D), jnp.float32)
    spare = jax.random.truncated_normal(whole_sequence_key, -4.0, 4.0, (D, D), jnp.float32)
    query_part = common / math.sqrt(D)
    key_part = spare / math.sqrt(D)
    return (jnp.clip(query_part, -4.0, 4.0), jnp.clip(key_part, -4.0, 4.0))


def draw_query_first(key, part):
    return weight_pair(key, 1)[0].astype(jnp.bfloat16)


def draw_key_first(key, part):
    return weight_pair(key, 1)[1].astype(jnp.bfloat16)


def draw_query_second(key, part):
    return weight_pair(key, 2)[0].astype(jnp.bfloat16)


def draw_key_second(key, part):
    return weight_pair(key, 2)[1].astype(jnp.bfloat16)


def touch_ends(values, key, low, top_value):
    extent = values.shape
    spot = [jax.random.randint(jax.random.fold_in(key, axis), (), 0, extent[axis]) for axis in range(len(extent))]
    values = values.at[tuple(spot)].set(low)
    longest = extent.index(max(extent))
    spot[longest] = (spot[longest] + 1) % extent[longest]
    return values.at[tuple(spot)].set(top_value)


def levels(stream_key, dims, cuts, smallest, high):
    def one(dim, shards_of):
        steps = jax.random.uniform(jax.random.fold_in(jax.random.fold_in(stream_key, 6), dim), (shards_of,), jnp.float32, smallest / len(cuts), high / len(cuts))
        return jnp.repeat(jnp.exp(steps), dims[dim] // shards_of).reshape((-1,) + (1,) * (len(dims) - dim - 1))

    level = one(*cuts[0])
    for cut in cuts[1:]:
        level = level * one(*cut)
    return level


def gaussian(own_key, shape, scale, bound, shards=(), held_as=jnp.bfloat16):
    factor_of = levels(own_key, shape, shards, -0.22, 0.18) if shards else 1.0
    drawn = jax.random.normal(own_key, shape, jnp.float32) * scale * factor_of
    return jnp.minimum(jnp.maximum(drawn, -bound), bound).astype(held_as)


def setup_inputs(seed: int = 0, part: int = 0) -> dict:
    key_list = jax.random.split(jax.random.key(seed), 17)
    part_splits = jax.random.split(jax.random.fold_in(key_list[16], part), 17)
    tokens = gaussian(part_splits[0], (TOKENS, D), 1.0, 6.0, ((0, 16),))
    attn_gain = jnp.clip(1.0 + 0.15 * jax.random.normal(key_list[1], (D,), jnp.float32), 0.25, 1.75)
    query_first = draw_query_first(jax.random.fold_in(key_list[16], 71), part)
    key_first = draw_key_first(jax.random.fold_in(key_list[16], 71), part)
    segment_value = gaussian(key_list[4], (D, D), D ** -0.5, 0.21875)
    output_first = gaussian(key_list[5], (D, D), HEAD_DIM ** -0.5, 0.875)
    mlp_gain = jnp.clip(1.0 + 0.15 * jax.random.normal(key_list[6], (D,), jnp.float32), 0.25, 1.75)
    up_weight = gaussian(key_list[7], (D, FF), D ** -0.5, 0.21875)
    down_weight = gaussian(key_list[8], (FF, D), FF ** -0.5, 0.109375)
    second_gain = jnp.clip(1.0 + 0.15 * jax.random.normal(key_list[9], (D,), jnp.float32), 0.25, 1.75)
    query_second = draw_query_second(jax.random.fold_in(key_list[16], 71), part)
    key_second = draw_key_second(jax.random.fold_in(key_list[16], 71), part)
    value_second = gaussian(key_list[12], (D, D), D ** -0.5, 0.21875)
    output_second = gaussian(key_list[13], (D, D), HEAD_DIM ** -0.5, 0.875)
    segment_offset = touch_ends(jax.random.randint(key_list[14], (HEADS,), 0, SEG_DEV * TOK_DEV // KEYS), jax.random.fold_in(key_list[14], 1), 0, (SEG_DEV * TOK_DEV // KEYS) - 1).astype(jnp.int32)
    global_offset = touch_ends(jax.random.randint(key_list[15], (HEADS,), 0, N_SEQ * TOK_DEV // KEYS), jax.random.fold_in(key_list[15], 1), 0, (N_SEQ * TOK_DEV // KEYS) - 1).astype(jnp.int32)
    return {"tokens": tokens, "attn_gain": attn_gain, "query_first": query_first, "key_first": key_first, "segment_value": segment_value, "output_first": output_first, "mlp_gain": mlp_gain, "up_weight": up_weight, "down_weight": down_weight, "second_gain": second_gain, "query_second": query_second, "key_second": key_second, "value_second": value_second, "output_second": output_second, "segment_offset": segment_offset, "global_offset": global_offset}


def norm_rows(values, gain):
    center = values - lax.optimization_barrier(jnp.mean(values, axis=-1, keepdims=True))
    spread = lax.optimization_barrier(jnp.mean(center * center, axis=-1, keepdims=True))
    return (center * lax.rsqrt(spread + 1e-05) * gain).astype(jnp.bfloat16)

def attend(query, keys, values):
    scores = jnp.einsum('thd,khd->htk', query.astype(jnp.float32), keys.astype(jnp.float32)) * HEAD_DIM ** (-0.5)
    highest = lax.optimization_barrier(jnp.max(scores, axis=-1, keepdims=True))
    weights = jnp.exp(scores - highest)
    weights = (weights / lax.optimization_barrier(jnp.sum(weights, axis=-1, keepdims=True))).astype(jnp.bfloat16)
    return jnp.einsum('htk,khd->thd', weights.astype(jnp.float32), values.astype(jnp.float32)).astype(jnp.bfloat16)

def project(chosen, weight):
    shaped = weight.astype(jnp.float32).reshape(D, HEADS, HEAD_DIM)
    return jnp.einsum('...hd,dhe->...he', chosen.astype(jnp.float32), shaped).astype(jnp.bfloat16)

def reference(tokens, attn_gain, query_first, key_first, segment_value, output_first, mlp_gain, up_weight, down_weight, second_gain, query_second, key_second, value_second, output_second, segment_offset, global_offset):
    seg_len = SEG_DEV * TOK_DEV
    segment_count = TOKENS // seg_len
    seg_rate = seg_len // KEYS
    hidden = norm_rows(tokens.astype(jnp.float32), attn_gain)
    query = jnp.dot(hidden, query_first, preferred_element_type=jnp.float32).astype(jnp.bfloat16)
    query = query.reshape(segment_count, seg_len, HEADS, HEAD_DIM)
    positions = (jnp.arange(segment_count, dtype=jnp.int32)[:, None, None] * seg_len + jnp.arange(KEYS, dtype=jnp.int32)[None, :, None] * seg_rate + segment_offset.astype(jnp.int32)[None, None, :]).astype(jnp.int32)
    chosen = hidden[positions]
    keys = project(chosen, key_first)
    values = project(chosen, segment_value)
    mixed = lax.map(lambda items: attend(items[0], items[1], items[2]), (query, keys, values)).reshape(TOKENS, D)
    first = (tokens.astype(jnp.float32) + jnp.dot(mixed, output_first, preferred_element_type=jnp.float32)).astype(jnp.bfloat16)
    normed = norm_rows(first.astype(jnp.float32), mlp_gain)
    inner = jax.nn.gelu(jnp.dot(normed, up_weight, preferred_element_type=jnp.float32), approximate=True).astype(jnp.bfloat16)
    second_branch = (first.astype(jnp.float32) + jnp.dot(inner, down_weight, preferred_element_type=jnp.float32)).astype(jnp.bfloat16)
    hidden_two = norm_rows(second_branch.astype(jnp.float32), second_gain)
    query_two = jnp.dot(hidden_two, query_second, preferred_element_type=jnp.float32).astype(jnp.bfloat16)
    query_two = query_two.reshape(segment_count, seg_len, HEADS, HEAD_DIM)
    glob_rate = TOKENS // KEYS
    positions_two = (jnp.arange(KEYS, dtype=jnp.int32)[:, None] * glob_rate + global_offset.astype(jnp.int32)[None, :]).astype(jnp.int32)
    chosen_two = hidden_two[positions_two]
    keys_two = project(chosen_two, key_second)
    values_two = project(chosen_two, value_second)
    mixed_two = lax.map(lambda block: attend(block, keys_two, values_two), query_two).reshape(TOKENS, D)
    return (second_branch.astype(jnp.float32) + jnp.dot(mixed_two, output_second, preferred_element_type=jnp.float32)).astype(jnp.bfloat16)
```

```python
import functools
import math

import jax
import jax.numpy as jnp
from jax import lax
from jax.experimental import pallas as pl
from jax.experimental.pallas import tpu as pltpu
from jax.sharding import PartitionSpec as P

KEYS = 256
SEG_MAX = 16


def swapped(x, axis, apart):
    return lax.ppermute(x, axis, [(i, i ^ 1 << apart) for i in range(lax.axis_size(axis))])


def norm_rows(values, gain):
    center = values - jnp.mean(values, axis=-1, keepdims=True)
    spread = jnp.mean(center * center, axis=-1, keepdims=True)
    return (center * lax.rsqrt(spread + 1e-05) * gain).astype(jnp.bfloat16)


def pick_keys(hidden, offsets, stride, key_weight, value_weight):
    token_count, width = hidden.shape
    head_count = offsets.shape[0]
    head_size = key_weight.shape[1] // head_count
    grouped_rows = hidden.reshape(token_count // stride, stride, width)
    dilation_selector = (
        lax.broadcasted_iota(jnp.int32, (stride, head_count), 0) == offsets[None, :]
    ).astype(jnp.bfloat16)
    chosen = jnp.einsum(
        "nof,oj->njf", grouped_rows, dilation_selector, preferred_element_type=jnp.float32
    ).astype(jnp.bfloat16)
    key_heads = jnp.einsum(
        "xkr,rkf->xkf",
        chosen,
        key_weight.reshape(width, head_count, head_size),
        preferred_element_type=jnp.float32,
    ).astype(jnp.bfloat16)
    value_heads = jnp.einsum(
        "xkr,rkf->xkf",
        chosen,
        value_weight.reshape(width, head_count, head_size),
        preferred_element_type=jnp.float32,
    ).astype(jnp.bfloat16)
    picked = token_count // stride
    return jnp.stack(
        [
            key_heads.reshape(picked, head_count * head_size),
            value_heads.reshape(picked, head_count * head_size),
        ]
    )


def attend_local(query, keyval, head_count):
    token_count, width = query.shape
    head_size = width // head_count
    query_heads = query.reshape(token_count, head_count, head_size)
    key_heads = keyval[0].reshape(-1, head_count, head_size)
    value_heads = keyval[1].reshape(-1, head_count, head_size)
    scores = jnp.einsum(
        "thd,khd->htk", query_heads, key_heads, preferred_element_type=jnp.float32
    ) * head_size ** (-0.5)
    highest = jnp.max(scores, axis=-1, keepdims=True)
    weights = jnp.exp(scores - highest)
    weights = (weights / jnp.sum(weights, axis=-1, keepdims=True)).astype(jnp.bfloat16)
    mixed = jnp.einsum(
        "htk,khd->thd", weights, value_heads, preferred_element_type=jnp.float32
    ).astype(jnp.bfloat16)
    return mixed.reshape(token_count, width)


def merge_branch_pair(mine, other, level, token_position):
    lower = token_position >> level & 1 == 0
    return jnp.where(
        lower, jnp.concatenate((mine, other), axis=1), jnp.concatenate((other, mine), axis=1)
    )


def spread_segment(keyval, seg_span, token_position):
    for level in range(seg_span.bit_length() - 1):
        partner = swapped(keyval, "seq", level)
        keyval = merge_branch_pair(keyval, partner, level, token_position)
    return keyval


def spread_global(keyval_two):
    keyval_two = lax.all_gather(keyval_two, "seq", axis=1, tiled=True)
    return keyval_two


def combine(partial_value, residual_full, need_full):
    row_count = residual_full.shape[0] // lax.axis_size("mp")
    row_start = lax.axis_index("mp") * row_count
    share = lax.psum_scatter(partial_value, "mp", scatter_dimension=0, tiled=True)
    own_rows = lax.dynamic_slice_in_dim(residual_full, row_start, row_count, 0)
    own_rows = (own_rows.astype(jnp.float32) + share).astype(jnp.bfloat16)
    full_rows = lax.all_gather(own_rows, "mp", axis=0, tiled=True) if need_full else own_rows
    return (own_rows, full_rows)


def body(
    tokens,
    attn_gain,
    query_first,
    key_first,
    segment_value,
    output_first,
    mlp_gain,
    up_weight,
    down_weight,
    second_gain,
    query_second,
    key_second,
    value_second,
    output_second,
    segment_offset,
    global_offset,
):
    seq_count = lax.axis_size("seq")
    token_position = lax.axis_index("seq")
    seg_span = min(SEG_MAX, seq_count)
    head_count = segment_offset.shape[0]
    full_rows = lax.all_gather(tokens, "mp", axis=0, tiled=True)
    token_count = full_rows.shape[0]
    hidden = norm_rows(full_rows.astype(jnp.float32), attn_gain)
    query = jnp.dot(hidden, query_first, preferred_element_type=jnp.float32).astype(jnp.bfloat16)
    seg_stride = token_count // (KEYS // seg_span)
    keyval = pick_keys(hidden, segment_offset, seg_stride, key_first, segment_value)
    keyval = spread_segment(keyval, seg_span, token_position)
    mixed = attend_local(query, keyval, head_count)
    partial_value = jnp.dot(mixed, output_first, preferred_element_type=jnp.float32)
    own_rows, first_rows = combine(partial_value, full_rows, True)
    normed = norm_rows(first_rows.astype(jnp.float32), mlp_gain)
    inner = jax.nn.gelu(
        jnp.dot(normed, up_weight, preferred_element_type=jnp.float32), approximate=True
    ).astype(jnp.bfloat16)
    partial_value = jnp.dot(inner, down_weight, preferred_element_type=jnp.float32)
    own_rows, second_rows = combine(partial_value, first_rows, True)
    hidden_two = norm_rows(second_rows.astype(jnp.float32), second_gain)
    query_two = jnp.dot(hidden_two, query_second, preferred_element_type=jnp.float32).astype(
        jnp.bfloat16
    )
    glob_stride = token_count // (KEYS // seq_count)
    keyval_two = pick_keys(hidden_two, global_offset, glob_stride, key_second, value_second)
    keyval_two = spread_global(keyval_two)
    mixed_two = attend_local(query_two, keyval_two, head_count)
    partial_value = jnp.dot(mixed_two, output_second, preferred_element_type=jnp.float32)
    own_rows, unused_rows = combine(partial_value, second_rows, False)
    return own_rows


MESH = pl.DeviceIdType.MESH
F32 = jnp.float32
BF16 = jnp.bfloat16
WINDOW = 256
LANES = 128


def iota(shape, axis):
    return lax.broadcasted_iota(jnp.int32, shape, axis)


def dot32(a, b):
    return jnp.dot(a, b, preferred_element_type=F32)


def gelu(x):
    return 0.5 * x * (1.0 + jnp.tanh(math.sqrt(2.0 / math.pi) * (x + 0.044715 * (x * x * x))))


class Gather:
    def __init__(self, n, buf, ssem, rsem):
        me = lax.axis_index("seq")
        self.me, self.n, self.high = me, n, n // 4
        self.buf, self.ssem, self.rsem = buf, ssem, rsem
        self.b0, self.b1, self.hi = me % 2, (me // 2) % 2, me // 4
        self.peer1 = self.hi * 4 + (1 - self.b1) * 2 + self.b0
        self.peer0 = self.hi * 4 + self.b1 * 2 + (1 - self.b0)

    def slot(self, d, b1, b0):
        return ((self.hi + self.high - d) % self.high) * 4 + b1 * 2 + b0

    def copy(self, slot, peer, k):
        return pltpu.make_async_remote_copy(
            src_ref=self.buf.at[slot],
            dst_ref=self.buf.at[slot],
            send_sem=self.ssem.at[k],
            recv_sem=self.rsem.at[slot],
            device_id={"seq": peer},
            device_id_type=MESH,
        )

    def peers(self):
        out = [((self.hi + d) % self.high) * 4 + self.b1 * 2 + self.b0 for d in range(1, self.high)]
        return out + [self.peer1, self.peer0]

    def start(self):
        h = self.high
        for d in range(1, h):
            peer = ((self.hi + d) % h) * 4 + self.b1 * 2 + self.b0
            self.copy(self.me, peer, d - 1).start()
        self.copy(self.me, self.peer1, h - 1).start()
        self.copy(self.me, self.peer0, 2 * h - 1).start()

    def second(self):
        h = self.high
        for d in range(1, h):
            slot = self.slot(d, self.b1, self.b0)
            self.copy(slot, self.peer1, h - 1 + d).wait_recv()
            self.copy(slot, self.peer1, h - 1 + d).start()
            self.copy(slot, self.peer0, 2 * h - 1 + d).start()

    def third(self):
        h = self.high
        for d in range(h):
            slot = self.slot(d, 1 - self.b1, self.b0)
            self.copy(slot, self.peer0, 3 * h - 1 + d).wait_recv()
            self.copy(slot, self.peer0, 3 * h - 1 + d).start()

    def finish(self):
        h = self.high
        for b1 in (self.b1, 1 - self.b1):
            for d in range(h):
                slot = self.slot(d, b1, 1 - self.b0)
                self.copy(slot, self.peer0, 0).wait_recv()
        for k in range(4 * h - 1):
            self.copy(self.me, self.peer0, k).wait_send()


def head_column(offset_ref, heads, picked):
    rows = iota((heads * picked, 1), 0) // picked
    column = jnp.zeros((heads * picked, 1), jnp.int32)
    for h in range(heads):
        column = jnp.where(rows == h, offset_ref[h], column)
    return column


def kernel(
    n, heads, picked, stride,
    seg_ref, glob_ref, x_ref, gain1_ref, gain_mlp_ref, gain2_ref,
    wq1_hbm, wk1_hbm, wv1_hbm, wo1_hbm, up_hbm, down_hbm, wq2_hbm, wk2_hbm, wv2_hbm, wo2_hbm,
    out_ref,
    wq1, wk1, wv1, wo1, up, down, wq2, wk2, wv2, wo2, wo_pad1, wo_pad2,
    xp, q, kv1, kv2, km, vp, perm, perm_back, mix, inner, sem, ssem1, rsem1, ssem2, rsem2,
):
    tokens, width = x_ref.shape
    size = width // heads
    half = LANES // 2
    chunk = heads * picked
    chunks = tokens // chunk
    keys = n * picked
    group = WINDOW // stride
    scale = size ** -0.5 * math.log2(math.e)

    pairs = [(wk1_hbm, wk1), (wv1_hbm, wv1), (wq1_hbm, wq1), (wo1_hbm, wo1), (up_hbm, up),
             (down_hbm, down), (wk2_hbm, wk2), (wv2_hbm, wv2), (wq2_hbm, wq2), (wo2_hbm, wo2)]
    loads = [pltpu.make_async_copy(a, b, sem.at[i]) for i, (a, b) in enumerate(pairs)]
    for load in loads:
        load.start()

    first_gather = Gather(n, kv1, ssem1, rsem1)
    second_gather = Gather(n, kv2, ssem2, rsem2)
    barrier = pltpu.get_barrier_semaphore()
    peers = first_gather.peers()
    for peer in peers:
        pl.semaphore_signal(barrier, inc=1, device_id={"seq": peer}, device_id_type=MESH)

    def own_heads(hidden, weight):
        full = dot32(hidden, weight[...])
        column = iota((picked, width), 1)
        total = jnp.zeros((picked, width), F32)
        for h in range(heads):
            mine = (column >= h * size) & (column < h * size + size)
            total = jnp.where(mine, full[h * picked:(h + 1) * picked], total)
        return total.astype(BF16)

    rows = iota((chunk, 1), 0)
    pick = rows % picked
    target = pick * stride + head_column(seg_ref, heads, picked)
    onehot = (iota((chunk, tokens), 1) == target).astype(F32).astype(BF16)
    hidden = norm_rows(dot32(onehot, x_ref[...]), gain1_ref[...])
    me = first_gather.me
    loads[0].wait()
    kv1[me, 0:picked, :] = own_heads(hidden, wk1)
    loads[1].wait()
    kv1[me, picked:2 * picked, :] = own_heads(hidden, wv1)
    pl.semaphore_wait(barrier, len(peers))
    first_gather.start()

    glob_col = head_column(glob_ref, heads, picked)
    lane = iota((16, WINDOW), 1)
    inside = lane % stride
    chosen = jnp.zeros((16, WINDOW), F32)
    for h in range(heads):
        chosen = jnp.where(inside == glob_ref[h], 1.0, chosen)
    a, b = iota((WINDOW, WINDOW), 0), iota((WINDOW, WINDOW), 1)
    same = a // stride == b // stride
    before = jnp.where(same & (a < b), 1.0, 0.0).astype(BF16)
    count = dot32(chosen.astype(BF16), before)
    total = dot32(chosen.astype(BF16), jnp.where(same, 1.0, 0.0).astype(BF16))
    rank = jnp.where(chosen > 0.5, count, total + inside.astype(F32) - count)
    rank_row = rank[0:1, :]
    table = jnp.where(same & (rank_row == (a % stride).astype(F32)), 1.0, 0.0)
    perm[...] = table.astype(BF16)
    perm_back[...] = table.T.astype(BF16)
    at_head = (iota((chunk, WINDOW), 1) == glob_col)
    head_rank = jnp.sum(jnp.where(at_head, rank_row, 0.0), axis=1, keepdims=True)
    spot = (pick * heads).astype(F32) + head_rank
    onehot_two = (iota((chunk, chunk), 1).astype(F32) == spot).astype(F32).astype(BF16)

    for g in range(tokens // WINDOW):
        moved = dot32(perm[...], x_ref[g * WINDOW:(g + 1) * WINDOW, :]).astype(BF16)
        for j in range(group):
            for c in range(chunks):
                at = c * chunk + (g * group + j) * heads
                xp[at:at + heads, :] = moved[j * stride + c * heads:j * stride + (c + 1) * heads]

    def window_of(h):
        return min(h * size // LANES * LANES, width - WINDOW)

    for h in range(heads):
        km[h] = jnp.zeros((WINDOW, keys), BF16)
        i = h % 2
        ones = iota((keys, LANES), 1) // half == i
        vp[h // 2, i * keys:(i + 1) * keys, LANES:] = jnp.where(ones, 1.0, 0.0).astype(BF16)
    for source, padded, load in ((wo1, wo_pad1, loads[3]), (wo2, wo_pad2, None)):
        if load is None:
            continue
        load.wait()
        for h in range(heads):
            padded[h * half:h * half + size, :] = source[h * size:(h + 1) * size, :]
            padded[h * half + size:(h + 1) * half, :] = jnp.zeros((half - size, width), BF16)

    first_gather.second()

    loads[2].wait()

    def query_chunk(c, carry):
        at = pl.ds(pl.multiple_of(c * chunk, chunk), chunk)
        hidden = norm_rows(xp[at, :].astype(F32), gain1_ref[...])
        q[at, :] = dot32(hidden, wq1[...]).astype(BF16)
        return carry

    lax.fori_loop(0, chunks, query_chunk, 0)
    first_gather.third()
    first_gather.finish()

    def set_keys(kv):
        key = kv[:, 0:picked, :].reshape(keys, width)
        value = kv[:, picked:2 * picked, :].reshape(keys, width)
        turned = key.astype(F32).T.astype(BF16)
        for h in range(heads):
            begin = h * size - window_of(h)
            km[h, begin:begin + size, :] = turned[h * size:(h + 1) * size, :]
            i = h % 2
            c, l = iota((WINDOW, LANES), 0) - begin, iota((WINDOW, LANES), 1) - i * half
            shift = jnp.where((c == l) & (l >= 0) & (l < size), 1.0, 0.0).astype(BF16)
            moved = dot32(value[:, window_of(h):window_of(h) + WINDOW], shift)
            vp[h // 2, i * keys:(i + 1) * keys, 0:LANES] = moved.astype(BF16)

    def attend(at):
        for pair in range(heads // 2):
            parts = []
            for h in (2 * pair, 2 * pair + 1):
                start = window_of(h)
                scores = dot32(q[at, start:start + WINDOW], km[h])
                top = jnp.max(scores, axis=-1, keepdims=True)
                parts.append(jnp.exp2((scores - top) * scale).astype(BF16))
            both = dot32(jnp.concatenate(parts, axis=1), vp[pair])
            mixed = both[:, :LANES] / both[:, LANES:]
            mix[:, pair * LANES:(pair + 1) * LANES] = mixed.astype(BF16)

    set_keys(kv1)
    loads[4].wait()
    loads[5].wait()
    loads[6].wait()
    loads[7].wait()
    loads[8].wait()

    def first_chunk(c, carry):
        at = pl.ds(pl.multiple_of(c * chunk, chunk), chunk)
        attend(at)
        first = (xp[at, :].astype(F32) + dot32(mix[...], wo_pad1[...])).astype(BF16)
        normed = norm_rows(first.astype(F32), gain_mlp_ref[...])
        hidden_units = up.shape[1]
        for start in range(0, hidden_units, width):
            part = dot32(normed, up[:, start:start + width])
            inner[:, start:start + width] = gelu(part).astype(BF16)
        second = (first.astype(F32) + dot32(inner[...], down[...])).astype(BF16)
        xp[at, :] = second
        hidden_two = norm_rows(second.astype(F32), gain2_ref[...])
        q[at, :] = dot32(hidden_two, wq2[...]).astype(BF16)

        @pl.when(c == 0)
        def _():
            picked_rows = dot32(onehot_two, hidden_two).astype(BF16)
            kv2[me, 0:picked, :] = own_heads(picked_rows, wk2)
            kv2[me, picked:2 * picked, :] = own_heads(picked_rows, wv2)
            second_gather.start()

        @pl.when(c == 1)
        def _():
            second_gather.second()

        @pl.when(c == 2)
        def _():
            second_gather.third()

        return carry

    lax.fori_loop(0, chunks, first_chunk, 0)
    loads[9].wait()
    for h in range(heads):
        wo_pad2[h * half:h * half + size, :] = wo2[h * size:(h + 1) * size, :]
        wo_pad2[h * half + size:(h + 1) * half, :] = jnp.zeros((half - size, width), BF16)
    second_gather.finish()
    set_keys(kv2)

    def last_chunk(c, carry):
        at = pl.ds(pl.multiple_of(c * chunk, chunk), chunk)
        attend(at)
        xp[at, :] = (xp[at, :].astype(F32) + dot32(mix[...], wo_pad2[...])).astype(BF16)
        return carry

    lax.fori_loop(0, chunks, last_chunk, 0)
    for g in range(tokens // WINDOW):
        blocks = []
        for j in range(group):
            for c in range(chunks):
                at = c * chunk + (g * group + j) * heads
                blocks.append(xp[at:at + heads, :])
        moved = dot32(perm_back[...], jnp.concatenate(blocks, axis=0))
        out_ref[g * WINDOW:(g + 1) * WINDOW, :] = moved.astype(BF16)


def whole_body(
    tokens, attn_gain, query_first, key_first, segment_value, output_first, mlp_gain, up_weight,
    down_weight, second_gain, query_second, key_second, value_second, output_second,
    segment_offset, global_offset,
):
    n = lax.axis_size("seq")
    heads = segment_offset.shape[0]
    picked = KEYS // n
    count, width = tokens.shape
    stride = count // picked
    units = up_weight.shape[1]
    chunk = heads * picked
    any_space = pl.BlockSpec(memory_space=pl.ANY)
    vmem = pl.BlockSpec(memory_space=pltpu.VMEM)
    smem = pl.BlockSpec(memory_space=pltpu.SMEM)
    square = pltpu.VMEM((width, width), BF16)
    padded = pltpu.VMEM((heads * LANES // 2, width), BF16)
    return pl.pallas_call(
        functools.partial(kernel, n, heads, picked, stride),
        out_shape=jax.ShapeDtypeStruct(tokens.shape, tokens.dtype),
        in_specs=[smem, smem, vmem, vmem, vmem, vmem] + [any_space] * 10,
        out_specs=vmem,
        scratch_shapes=[
            square, square, square, square,
            pltpu.VMEM((width, units), BF16), pltpu.VMEM((units, width), BF16),
            square, square, square, square, padded, padded,
            pltpu.VMEM((count, width), BF16),
            pltpu.VMEM((count, width), BF16),
            pltpu.VMEM((n, 2 * picked, width), BF16),
            pltpu.VMEM((n, 2 * picked, width), BF16),
            pltpu.VMEM((heads, WINDOW, KEYS), BF16),
            pltpu.VMEM((heads // 2, 2 * KEYS, 2 * LANES), BF16),
            pltpu.VMEM((WINDOW, WINDOW), BF16),
            pltpu.VMEM((WINDOW, WINDOW), BF16),
            pltpu.VMEM((chunk, heads * LANES // 2), BF16),
            pltpu.VMEM((chunk, units), BF16),
            pltpu.SemaphoreType.DMA((10,)),
            pltpu.SemaphoreType.DMA((n,)), pltpu.SemaphoreType.DMA((n,)),
            pltpu.SemaphoreType.DMA((n,)), pltpu.SemaphoreType.DMA((n,)),
        ],
        compiler_params=pltpu.CompilerParams(
            collective_id=0, has_side_effects=True, vmem_limit_bytes=60 << 20
        ),
        name="encoder",
    )(
        segment_offset, global_offset, tokens, attn_gain[None], mlp_gain[None], second_gain[None],
        query_first, key_first, segment_value, output_first, up_weight, down_weight,
        query_second, key_second, value_second, output_second,
    )


def fits(mesh):
    n = mesh.shape["seq"]
    return mesh.shape["mp"] == 1 and n == SEG_MAX


def choose(mesh):
    return whole_body if fits(mesh) else body


def solution(mesh):
    placed = (
        P(("slides", "seq", "mp"), None),
        P(),
        P(None, "mp"),
        P(None, "mp"),
        P(None, "mp"),
        P("mp", None),
        P(),
        P(None, "mp"),
        P("mp", None),
        P(),
        P(None, "mp"),
        P(None, "mp"),
        P(None, "mp"),
        P("mp", None),
        P("mp"),
        P("mp"),
    )
    return jax.shard_map(
        choose(mesh),
        mesh=mesh,
        in_specs=placed,
        out_specs=P(("slides", "seq", "mp"), None),
        check_vma=False,
    )
```

```python
import functools
import math

import jax
import jax.numpy as jnp
from jax import lax
from jax.experimental import pallas as pl
from jax.experimental.pallas import tpu as pltpu
from jax.sharding import PartitionSpec as P

KEYS = 256
SEG_MAX = 16


def swapped(x, axis, apart):
    return lax.ppermute(x, axis, [(i, i ^ 1 << apart) for i in range(lax.axis_size(axis))])


def norm_rows(values, gain):
    center = values - jnp.mean(values, axis=-1, keepdims=True)
    spread = jnp.mean(center * center, axis=-1, keepdims=True)
    return (center * lax.rsqrt(spread + 1e-05) * gain).astype(jnp.bfloat16)


def pick_keys(hidden, offsets, stride, key_weight, value_weight):
    token_count, width = hidden.shape
    head_count = offsets.shape[0]
    head_size = key_weight.shape[1] // head_count
    grouped_rows = hidden.reshape(token_count // stride, stride, width)
    dilation_selector = (
        lax.broadcasted_iota(jnp.int32, (stride, head_count), 0) == offsets[None, :]
    ).astype(jnp.bfloat16)
    chosen = jnp.einsum(
        "nof,oj->njf", grouped_rows, dilation_selector, preferred_element_type=jnp.float32
    ).astype(jnp.bfloat16)
    key_heads = jnp.einsum(
        "xkr,rkf->xkf",
        chosen,
        key_weight.reshape(width, head_count, head_size),
        preferred_element_type=jnp.float32,
    ).astype(jnp.bfloat16)
    value_heads = jnp.einsum(
        "xkr,rkf->xkf",
        chosen,
        value_weight.reshape(width, head_count, head_size),
        preferred_element_type=jnp.float32,
    ).astype(jnp.bfloat16)
    picked = token_count // stride
    return jnp.stack(
        [
            key_heads.reshape(picked, head_count * head_size),
            value_heads.reshape(picked, head_count * head_size),
        ]
    )


def attend_local(query, keyval, head_count):
    token_count, width = query.shape
    head_size = width // head_count
    query_heads = query.reshape(token_count, head_count, head_size)
    key_heads = keyval[0].reshape(-1, head_count, head_size)
    value_heads = keyval[1].reshape(-1, head_count, head_size)
    scores = jnp.einsum(
        "thd,khd->htk", query_heads, key_heads, preferred_element_type=jnp.float32
    ) * head_size ** (-0.5)
    highest = jnp.max(scores, axis=-1, keepdims=True)
    weights = jnp.exp(scores - highest)
    weights = (weights / jnp.sum(weights, axis=-1, keepdims=True)).astype(jnp.bfloat16)
    mixed = jnp.einsum(
        "htk,khd->thd", weights, value_heads, preferred_element_type=jnp.float32
    ).astype(jnp.bfloat16)
    return mixed.reshape(token_count, width)


def merge_branch_pair(mine, other, level, token_position):
    lower = token_position >> level & 1 == 0
    return jnp.where(
        lower, jnp.concatenate((mine, other), axis=1), jnp.concatenate((other, mine), axis=1)
    )


def spread_segment(keyval, seg_span, token_position):
    for level in range(seg_span.bit_length() - 1):
        partner = swapped(keyval, "seq", level)
        keyval = merge_branch_pair(keyval, partner, level, token_position)
    return keyval


def spread_global(keyval_two):
    keyval_two = lax.all_gather(keyval_two, "seq", axis=1, tiled=True)
    return keyval_two


def combine(partial_value, residual_full, need_full):
    row_count = residual_full.shape[0] // lax.axis_size("mp")
    row_start = lax.axis_index("mp") * row_count
    share = lax.psum_scatter(partial_value, "mp", scatter_dimension=0, tiled=True)
    own_rows = lax.dynamic_slice_in_dim(residual_full, row_start, row_count, 0)
    own_rows = (own_rows.astype(jnp.float32) + share).astype(jnp.bfloat16)
    full_rows = lax.all_gather(own_rows, "mp", axis=0, tiled=True) if need_full else own_rows
    return (own_rows, full_rows)


def body(
    tokens,
    attn_gain,
    query_first,
    key_first,
    segment_value,
    output_first,
    mlp_gain,
    up_weight,
    down_weight,
    second_gain,
    query_second,
    key_second,
    value_second,
    output_second,
    segment_offset,
    global_offset,
):
    seq_count = lax.axis_size("seq")
    token_position = lax.axis_index("seq")
    seg_span = min(SEG_MAX, seq_count)
    head_count = segment_offset.shape[0]
    full_rows = lax.all_gather(tokens, "mp", axis=0, tiled=True)
    token_count = full_rows.shape[0]
    hidden = norm_rows(full_rows.astype(jnp.float32), attn_gain)
    query = jnp.dot(hidden, query_first, preferred_element_type=jnp.float32).astype(jnp.bfloat16)
    seg_stride = token_count // (KEYS // seg_span)
    keyval = pick_keys(hidden, segment_offset, seg_stride, key_first, segment_value)
    keyval = spread_segment(keyval, seg_span, token_position)
    mixed = attend_local(query, keyval, head_count)
    partial_value = jnp.dot(mixed, output_first, preferred_element_type=jnp.float32)
    own_rows, first_rows = combine(partial_value, full_rows, True)
    normed = norm_rows(first_rows.astype(jnp.float32), mlp_gain)
    inner = jax.nn.gelu(
        jnp.dot(normed, up_weight, preferred_element_type=jnp.float32), approximate=True
    ).astype(jnp.bfloat16)
    partial_value = jnp.dot(inner, down_weight, preferred_element_type=jnp.float32)
    own_rows, second_rows = combine(partial_value, first_rows, True)
    hidden_two = norm_rows(second_rows.astype(jnp.float32), second_gain)
    query_two = jnp.dot(hidden_two, query_second, preferred_element_type=jnp.float32).astype(
        jnp.bfloat16
    )
    glob_stride = token_count // (KEYS // seq_count)
    keyval_two = pick_keys(hidden_two, global_offset, glob_stride, key_second, value_second)
    keyval_two = spread_global(keyval_two)
    mixed_two = attend_local(query_two, keyval_two, head_count)
    partial_value = jnp.dot(mixed_two, output_second, preferred_element_type=jnp.float32)
    own_rows, unused_rows = combine(partial_value, second_rows, False)
    return own_rows


MESH = pl.DeviceIdType.MESH
F32 = jnp.float32
BF16 = jnp.bfloat16
WINDOW = 256
LANES = 128


def iota(shape, axis):
    return lax.broadcasted_iota(jnp.int32, shape, axis)


def dot32(a, b):
    return jnp.dot(a, b, preferred_element_type=F32)


def gelu(x):
    return 0.5 * x * (1.0 + jnp.tanh(math.sqrt(2.0 / math.pi) * (x + 0.044715 * (x * x * x))))


class Gather:
    def __init__(self, n, buf, ssem, rsem):
        me = lax.axis_index("seq")
        self.me, self.n, self.high = me, n, n // 4
        self.buf, self.ssem, self.rsem = buf, ssem, rsem
        self.b0, self.b1, self.hi = me % 2, (me // 2) % 2, me // 4
        self.peer1 = self.hi * 4 + (1 - self.b1) * 2 + self.b0
        self.peer0 = self.hi * 4 + self.b1 * 2 + (1 - self.b0)

    def slot(self, d, b1, b0):
        return ((self.hi + self.high - d) % self.high) * 4 + b1 * 2 + b0

    def copy(self, slot, peer, k):
        return pltpu.make_async_remote_copy(
            src_ref=self.buf.at[slot],
            dst_ref=self.buf.at[slot],
            send_sem=self.ssem.at[k],
            recv_sem=self.rsem.at[slot],
            device_id={"seq": peer},
            device_id_type=MESH,
        )

    def peers(self):
        out = [((self.hi + d) % self.high) * 4 + self.b1 * 2 + self.b0 for d in range(1, self.high)]
        return out + [self.peer1, self.peer0]

    def start(self):
        h = self.high
        for d in range(1, h):
            peer = ((self.hi + d) % h) * 4 + self.b1 * 2 + self.b0
            self.copy(self.me, peer, d - 1).start()
        self.copy(self.me, self.peer1, h - 1).start()
        self.copy(self.me, self.peer0, 2 * h - 1).start()

    def second(self):
        h = self.high
        for d in range(1, h):
            slot = self.slot(d, self.b1, self.b0)
            self.copy(slot, self.peer1, h - 1 + d).wait_recv()
            self.copy(slot, self.peer1, h - 1 + d).start()
            self.copy(slot, self.peer0, 2 * h - 1 + d).start()

    def third(self):
        h = self.high
        for d in range(h):
            slot = self.slot(d, 1 - self.b1, self.b0)
            self.copy(slot, self.peer0, 3 * h - 1 + d).wait_recv()
            self.copy(slot, self.peer0, 3 * h - 1 + d).start()

    def finish(self):
        h = self.high
        for b1 in (self.b1, 1 - self.b1):
            for d in range(h):
                slot = self.slot(d, b1, 1 - self.b0)
                self.copy(slot, self.peer0, 0).wait_recv()
        for k in range(4 * h - 1):
            self.copy(self.me, self.peer0, k).wait_send()


def head_column(offset_ref, heads, picked):
    rows = iota((heads * picked, 1), 0) // picked
    column = jnp.zeros((heads * picked, 1), jnp.int32)
    for h in range(heads):
        column = jnp.where(rows == h, offset_ref[h], column)
    return column


def kernel(
    n, heads, picked, stride,
    seg_ref, glob_ref, x_ref, gain1_ref, gain_mlp_ref, gain2_ref,
    wq1_hbm, wk1_hbm, wv1_hbm, wo1_hbm, up_hbm, down_hbm, wq2_hbm, wk2_hbm, wv2_hbm, wo2_hbm,
    out_ref,
    wq1, wk1, wv1, wo1, up, down, wq2, wk2, wv2, wo2, wo_pad1, wo_pad2,
    xp, q, kv1, kv2, km, vp, perm, perm_back, mix, inner, sem, ssem1, rsem1, ssem2, rsem2,
):
    tokens, width = x_ref.shape
    size = width // heads
    half = LANES // 2
    chunk = heads * picked
    chunks = tokens // chunk
    keys = n * picked
    group = WINDOW // stride
    scale = size ** -0.5 * math.log2(math.e)

    pairs = [(wk1_hbm, wk1), (wv1_hbm, wv1), (wq1_hbm, wq1), (wo1_hbm, wo1), (up_hbm, up),
             (down_hbm, down), (wk2_hbm, wk2), (wv2_hbm, wv2), (wq2_hbm, wq2), (wo2_hbm, wo2)]
    loads = [pltpu.make_async_copy(a, b, sem.at[i]) for i, (a, b) in enumerate(pairs)]
    for load in loads:
        load.start()

    first_gather = Gather(n, kv1, ssem1, rsem1)
    second_gather = Gather(n, kv2, ssem2, rsem2)
    barrier = pltpu.get_barrier_semaphore()
    peers = first_gather.peers()
    for peer in peers:
        pl.semaphore_signal(barrier, inc=1, device_id={"seq": peer}, device_id_type=MESH)

    def own_heads(hidden, weight):
        full = dot32(hidden, weight[...])
        column = iota((picked, width), 1)
        total = jnp.zeros((picked, width), F32)
        for h in range(heads):
            mine = (column >= h * size) & (column < h * size + size)
            total = jnp.where(mine, full[h * picked:(h + 1) * picked], total)
        return total.astype(BF16)

    rows = iota((chunk, 1), 0)
    pick = rows % picked
    target = pick * stride + head_column(seg_ref, heads, picked)
    onehot = (iota((chunk, tokens), 1) == target).astype(F32).astype(BF16)
    hidden = norm_rows(dot32(onehot, x_ref[...]), gain1_ref[...][None, :])
    me = first_gather.me
    loads[0].wait()
    kv1[me, 0:picked, :] = own_heads(hidden, wk1)
    loads[1].wait()
    kv1[me, picked:2 * picked, :] = own_heads(hidden, wv1)
    pl.semaphore_wait(barrier, len(peers))
    first_gather.start()

    glob_col = head_column(glob_ref, heads, picked)
    lane = iota((16, WINDOW), 1)
    inside = lane % stride
    chosen = jnp.zeros((16, WINDOW), F32)
    for h in range(heads):
        chosen = jnp.where(inside == glob_ref[h], 1.0, chosen)
    a, b = iota((WINDOW, WINDOW), 0), iota((WINDOW, WINDOW), 1)
    same = a // stride == b // stride
    before = jnp.where(same & (a < b), 1.0, 0.0).astype(BF16)
    count = dot32(chosen.astype(BF16), before)
    total = dot32(chosen.astype(BF16), jnp.where(same, 1.0, 0.0).astype(BF16))
    rank = jnp.where(chosen > 0.5, count, total + inside.astype(F32) - count)
    rank_row = rank[0:1, :]
    table = jnp.where(same & (rank_row == (a % stride).astype(F32)), 1.0, 0.0)
    perm[...] = table.astype(BF16)
    perm_back[...] = table.T.astype(BF16)
    at_head = (iota((chunk, WINDOW), 1) == glob_col)
    head_rank = jnp.sum(jnp.where(at_head, rank_row, 0.0), axis=1, keepdims=True)
    spot = (pick * heads).astype(F32) + head_rank
    onehot_two = (iota((chunk, chunk), 1).astype(F32) == spot).astype(F32).astype(BF16)

    for g in range(tokens // WINDOW):
        moved = dot32(perm[...], x_ref[g * WINDOW:(g + 1) * WINDOW, :]).astype(BF16)
        for j in range(group):
            for c in range(chunks):
                at = c * chunk + (g * group + j) * heads
                xp[at:at + heads, :] = moved[j * stride + c * heads:j * stride + (c + 1) * heads]

    def window_of(h):
        return min(h * size // LANES * LANES, width - WINDOW)

    for h in range(heads):
        km[h] = jnp.zeros((WINDOW, keys), BF16)
        i = h % 2
        ones = iota((keys, LANES), 1) // half == i
        vp[h // 2, i * keys:(i + 1) * keys, LANES:] = jnp.where(ones, 1.0, 0.0).astype(BF16)
    for source, padded, load in ((wo1, wo_pad1, loads[3]), (wo2, wo_pad2, None)):
        if load is None:
            continue
        load.wait()
        for h in range(heads):
            padded[h * half:h * half + size, :] = source[h * size:(h + 1) * size, :]
            padded[h * half + size:(h + 1) * half, :] = jnp.zeros((half - size, width), BF16)

    first_gather.second()

    loads[2].wait()

    def query_chunk(c, carry):
        at = pl.ds(pl.multiple_of(c * chunk, chunk), chunk)
        hidden = norm_rows(xp[at, :].astype(F32), gain1_ref[...][None, :])
        q[at, :] = dot32(hidden, wq1[...]).astype(BF16)
        return carry

    lax.fori_loop(0, chunks, query_chunk, 0)
    first_gather.third()
    first_gather.finish()

    def set_keys(kv):
        key = kv[:, 0:picked, :].reshape(keys, width)
        value = kv[:, picked:2 * picked, :].reshape(keys, width)
        turned = key.astype(F32).T.astype(BF16)
        for h in range(heads):
            begin = h * size - window_of(h)
            km[h, begin:begin + size, :] = turned[h * size:(h + 1) * size, :]
            i = h % 2
            c, l = iota((WINDOW, LANES), 0) - begin, iota((WINDOW, LANES), 1) - i * half
            shift = jnp.where((c == l) & (l >= 0) & (l < size), 1.0, 0.0).astype(BF16)
            moved = dot32(value[:, window_of(h):window_of(h) + WINDOW], shift)
            vp[h // 2, i * keys:(i + 1) * keys, 0:LANES] = moved.astype(BF16)

    def attend(at):
        for pair in range(heads // 2):
            parts = []
            for h in (2 * pair, 2 * pair + 1):
                start = window_of(h)
                scores = dot32(q[at, start:start + WINDOW], km[h])
                top = jnp.max(scores, axis=-1, keepdims=True)
                parts.append(jnp.exp2((scores - top) * scale).astype(BF16))
            both = dot32(jnp.concatenate(parts, axis=1), vp[pair])
            mixed = both[:, :LANES] / both[:, LANES:]
            mix[:, pair * LANES:(pair + 1) * LANES] = mixed.astype(BF16)

    set_keys(kv1)
    loads[4].wait()
    loads[5].wait()
    loads[6].wait()
    loads[7].wait()
    loads[8].wait()

    def first_chunk(c, carry):
        at = pl.ds(pl.multiple_of(c * chunk, chunk), chunk)
        attend(at)
        first = (xp[at, :].astype(F32) + dot32(mix[...], wo_pad1[...])).astype(BF16)
        normed = norm_rows(first.astype(F32), gain_mlp_ref[...][None, :])
        hidden_units = up.shape[1]
        for start in range(0, hidden_units, width):
            part = dot32(normed, up[:, start:start + width])
            inner[:, start:start + width] = gelu(part).astype(BF16)
        second = (first.astype(F32) + dot32(inner[...], down[...])).astype(BF16)
        xp[at, :] = second
        hidden_two = norm_rows(second.astype(F32), gain2_ref[...][None, :])
        q[at, :] = dot32(hidden_two, wq2[...]).astype(BF16)

        @pl.when(c == 0)
        def _():
            picked_rows = dot32(onehot_two, hidden_two).astype(BF16)
            kv2[me, 0:picked, :] = own_heads(picked_rows, wk2)
            kv2[me, picked:2 * picked, :] = own_heads(picked_rows, wv2)
            second_gather.start()

        @pl.when(c == 1)
        def _():
            second_gather.second()

        @pl.when(c == 2)
        def _():
            second_gather.third()

        return carry

    lax.fori_loop(0, chunks, first_chunk, 0)
    loads[9].wait()
    for h in range(heads):
        wo_pad2[h * half:h * half + size, :] = wo2[h * size:(h + 1) * size, :]
        wo_pad2[h * half + size:(h + 1) * half, :] = jnp.zeros((half - size, width), BF16)
    second_gather.finish()
    set_keys(kv2)

    def last_chunk(c, carry):
        at = pl.ds(pl.multiple_of(c * chunk, chunk), chunk)
        attend(at)
        xp[at, :] = (xp[at, :].astype(F32) + dot32(mix[...], wo_pad2[...])).astype(BF16)
        return carry

    lax.fori_loop(0, chunks, last_chunk, 0)
    for g in range(tokens // WINDOW):
        blocks = []
        for j in range(group):
            for c in range(chunks):
                at = c * chunk + (g * group + j) * heads
                blocks.append(xp[at:at + heads, :])
        moved = dot32(perm_back[...], jnp.concatenate(blocks, axis=0))
        out_ref[g * WINDOW:(g + 1) * WINDOW, :] = moved.astype(BF16)


def whole_body(
    tokens, attn_gain, query_first, key_first, segment_value, output_first, mlp_gain, up_weight,
    down_weight, second_gain, query_second, key_second, value_second, output_second,
    segment_offset, global_offset,
):
    n = lax.axis_size("seq")
    heads = segment_offset.shape[0]
    picked = KEYS // n
    count, width = tokens.shape
    stride = count // picked
    units = up_weight.shape[1]
    chunk = heads * picked
    any_space = pl.BlockSpec(memory_space=pl.ANY)
    vmem = pl.BlockSpec(memory_space=pltpu.VMEM)
    smem = pl.BlockSpec(memory_space=pltpu.SMEM)
    square = pltpu.VMEM((width, width), BF16)
    padded = pltpu.VMEM((heads * LANES // 2, width), BF16)
    return pl.pallas_call(
        functools.partial(kernel, n, heads, picked, stride),
        out_shape=jax.ShapeDtypeStruct(tokens.shape, tokens.dtype),
        in_specs=[smem, smem, vmem, vmem, vmem, vmem] + [any_space] * 10,
        out_specs=vmem,
        scratch_shapes=[
            square, square, square, square,
            pltpu.VMEM((width, units), BF16), pltpu.VMEM((units, width), BF16),
            square, square, square, square, padded, padded,
            pltpu.VMEM((count, width), BF16),
            pltpu.VMEM((count, width), BF16),
            pltpu.VMEM((n, 2 * picked, width), BF16),
            pltpu.VMEM((n, 2 * picked, width), BF16),
            pltpu.VMEM((heads, WINDOW, KEYS), BF16),
            pltpu.VMEM((heads // 2, 2 * KEYS, 2 * LANES), BF16),
            pltpu.VMEM((WINDOW, WINDOW), BF16),
            pltpu.VMEM((WINDOW, WINDOW), BF16),
            pltpu.VMEM((chunk, heads * LANES // 2), BF16),
            pltpu.VMEM((chunk, units), BF16),
            pltpu.SemaphoreType.DMA((10,)),
            pltpu.SemaphoreType.DMA((n,)), pltpu.SemaphoreType.DMA((n,)),
            pltpu.SemaphoreType.DMA((n,)), pltpu.SemaphoreType.DMA((n,)),
        ],
        compiler_params=pltpu.CompilerParams(
            collective_id=0, has_side_effects=True, vmem_limit_bytes=60 << 20
        ),
        name="encoder",
    )(
        segment_offset, global_offset, tokens, attn_gain, mlp_gain, second_gain,
        query_first, key_first, segment_value, output_first, up_weight, down_weight,
        query_second, key_second, value_second, output_second,
    )


def fits(mesh):
    n = mesh.shape["seq"]
    return mesh.shape["mp"] == 1 and n == SEG_MAX


def choose(mesh):
    return whole_body if fits(mesh) else body


def solution(mesh):
    placed = (
        P(("slides", "seq", "mp"), None),
        P(),
        P(None, "mp"),
        P(None, "mp"),
        P(None, "mp"),
        P("mp", None),
        P(),
        P(None, "mp"),
        P("mp", None),
        P(),
        P(None, "mp"),
        P(None, "mp"),
        P(None, "mp"),
        P("mp", None),
        P("mp"),
        P("mp"),
    )
    return jax.shard_map(
        choose(mesh),
        mesh=mesh,
        in_specs=placed,
        out_specs=P(("slides", "seq", "mp"), None),
        check_vma=False,
    )
```

```python
import functools
import math

import jax
import jax.numpy as jnp
from jax import lax
from jax.experimental import pallas as pl
from jax.experimental.pallas import tpu as pltpu
from jax.sharding import PartitionSpec as P

KEYS = 256
SEG_MAX = 16


def swapped(x, axis, apart):
    return lax.ppermute(x, axis, [(i, i ^ 1 << apart) for i in range(lax.axis_size(axis))])


def norm_rows(values, gain):
    center = values - jnp.mean(values, axis=-1, keepdims=True)
    spread = jnp.mean(center * center, axis=-1, keepdims=True)
    return (center * lax.rsqrt(spread + 1e-05) * gain).astype(jnp.bfloat16)


def pick_keys(hidden, offsets, stride, key_weight, value_weight):
    token_count, width = hidden.shape
    head_count = offsets.shape[0]
    head_size = key_weight.shape[1] // head_count
    grouped_rows = hidden.reshape(token_count // stride, stride, width)
    dilation_selector = (
        lax.broadcasted_iota(jnp.int32, (stride, head_count), 0) == offsets[None, :]
    ).astype(jnp.bfloat16)
    chosen = jnp.einsum(
        "nof,oj->njf", grouped_rows, dilation_selector, preferred_element_type=jnp.float32
    ).astype(jnp.bfloat16)
    key_heads = jnp.einsum(
        "xkr,rkf->xkf",
        chosen,
        key_weight.reshape(width, head_count, head_size),
        preferred_element_type=jnp.float32,
    ).astype(jnp.bfloat16)
    value_heads = jnp.einsum(
        "xkr,rkf->xkf",
        chosen,
        value_weight.reshape(width, head_count, head_size),
        preferred_element_type=jnp.float32,
    ).astype(jnp.bfloat16)
    picked = token_count // stride
    return jnp.stack(
        [
            key_heads.reshape(picked, head_count * head_size),
            value_heads.reshape(picked, head_count * head_size),
        ]
    )


def attend_local(query, keyval, head_count):
    token_count, width = query.shape
    head_size = width // head_count
    query_heads = query.reshape(token_count, head_count, head_size)
    key_heads = keyval[0].reshape(-1, head_count, head_size)
    value_heads = keyval[1].reshape(-1, head_count, head_size)
    scores = jnp.einsum(
        "thd,khd->htk", query_heads, key_heads, preferred_element_type=jnp.float32
    ) * head_size ** (-0.5)
    highest = jnp.max(scores, axis=-1, keepdims=True)
    weights = jnp.exp(scores - highest)
    weights = (weights / jnp.sum(weights, axis=-1, keepdims=True)).astype(jnp.bfloat16)
    mixed = jnp.einsum(
        "htk,khd->thd", weights, value_heads, preferred_element_type=jnp.float32
    ).astype(jnp.bfloat16)
    return mixed.reshape(token_count, width)


def merge_branch_pair(mine, other, level, token_position):
    lower = token_position >> level & 1 == 0
    return jnp.where(
        lower, jnp.concatenate((mine, other), axis=1), jnp.concatenate((other, mine), axis=1)
    )


def spread_segment(keyval, seg_span, token_position):
    for level in range(seg_span.bit_length() - 1):
        partner = swapped(keyval, "seq", level)
        keyval = merge_branch_pair(keyval, partner, level, token_position)
    return keyval


def spread_global(keyval_two):
    keyval_two = lax.all_gather(keyval_two, "seq", axis=1, tiled=True)
    return keyval_two


def combine(partial_value, residual_full, need_full):
    row_count = residual_full.shape[0] // lax.axis_size("mp")
    row_start = lax.axis_index("mp") * row_count
    share = lax.psum_scatter(partial_value, "mp", scatter_dimension=0, tiled=True)
    own_rows = lax.dynamic_slice_in_dim(residual_full, row_start, row_count, 0)
    own_rows = (own_rows.astype(jnp.float32) + share).astype(jnp.bfloat16)
    full_rows = lax.all_gather(own_rows, "mp", axis=0, tiled=True) if need_full else own_rows
    return (own_rows, full_rows)


def body(
    tokens,
    attn_gain,
    query_first,
    key_first,
    segment_value,
    output_first,
    mlp_gain,
    up_weight,
    down_weight,
    second_gain,
    query_second,
    key_second,
    value_second,
    output_second,
    segment_offset,
    global_offset,
):
    seq_count = lax.axis_size("seq")
    token_position = lax.axis_index("seq")
    seg_span = min(SEG_MAX, seq_count)
    head_count = segment_offset.shape[0]
    full_rows = lax.all_gather(tokens, "mp", axis=0, tiled=True)
    token_count = full_rows.shape[0]
    hidden = norm_rows(full_rows.astype(jnp.float32), attn_gain)
    query = jnp.dot(hidden, query_first, preferred_element_type=jnp.float32).astype(jnp.bfloat16)
    seg_stride = token_count // (KEYS // seg_span)
    keyval = pick_keys(hidden, segment_offset, seg_stride, key_first, segment_value)
    keyval = spread_segment(keyval, seg_span, token_position)
    mixed = attend_local(query, keyval, head_count)
    partial_value = jnp.dot(mixed, output_first, preferred_element_type=jnp.float32)
    own_rows, first_rows = combine(partial_value, full_rows, True)
    normed = norm_rows(first_rows.astype(jnp.float32), mlp_gain)
    inner = jax.nn.gelu(
        jnp.dot(normed, up_weight, preferred_element_type=jnp.float32), approximate=True
    ).astype(jnp.bfloat16)
    partial_value = jnp.dot(inner, down_weight, preferred_element_type=jnp.float32)
    own_rows, second_rows = combine(partial_value, first_rows, True)
    hidden_two = norm_rows(second_rows.astype(jnp.float32), second_gain)
    query_two = jnp.dot(hidden_two, query_second, preferred_element_type=jnp.float32).astype(
        jnp.bfloat16
    )
    glob_stride = token_count // (KEYS // seq_count)
    keyval_two = pick_keys(hidden_two, global_offset, glob_stride, key_second, value_second)
    keyval_two = spread_global(keyval_two)
    mixed_two = attend_local(query_two, keyval_two, head_count)
    partial_value = jnp.dot(mixed_two, output_second, preferred_element_type=jnp.float32)
    own_rows, unused_rows = combine(partial_value, second_rows, False)
    return own_rows


MESH = pl.DeviceIdType.MESH
F32 = jnp.float32
BF16 = jnp.bfloat16
WINDOW = 256
LANES = 128
VMEM_BYTES = 62 << 20


def iota(shape, axis):
    return lax.broadcasted_iota(jnp.int32, shape, axis)


def dot32(a, b):
    return jnp.dot(a, b, preferred_element_type=F32)


def gelu(x):
    return 0.5 * x * (1.0 + jnp.tanh(math.sqrt(2.0 / math.pi) * (x + 0.044715 * (x * x * x))))


class Gather:
    def __init__(self, n, buf, ssem, rsem):
        me = lax.axis_index("seq")
        self.me, self.n, self.high = me, n, n // 4
        self.buf, self.ssem, self.rsem = buf, ssem, rsem
        self.b0, self.b1, self.hi = me % 2, (me // 2) % 2, me // 4
        self.peer1 = self.hi * 4 + (1 - self.b1) * 2 + self.b0
        self.peer0 = self.hi * 4 + self.b1 * 2 + (1 - self.b0)

    def slot(self, d, b1, b0):
        return ((self.hi + self.high - d) % self.high) * 4 + b1 * 2 + b0

    def copy(self, slot, peer, k):
        return pltpu.make_async_remote_copy(
            src_ref=self.buf.at[slot],
            dst_ref=self.buf.at[slot],
            send_sem=self.ssem.at[k],
            recv_sem=self.rsem.at[slot],
            device_id={"seq": peer},
            device_id_type=MESH,
        )

    def peers(self):
        out = [((self.hi + d) % self.high) * 4 + self.b1 * 2 + self.b0 for d in range(1, self.high)]
        return out + [self.peer1, self.peer0]

    def start(self):
        h = self.high
        for d in range(1, h):
            peer = ((self.hi + d) % h) * 4 + self.b1 * 2 + self.b0
            self.copy(self.me, peer, d - 1).start()
        self.copy(self.me, self.peer1, h - 1).start()
        self.copy(self.me, self.peer0, 2 * h - 1).start()

    def second(self):
        h = self.high
        for d in range(1, h):
            slot = self.slot(d, self.b1, self.b0)
            self.copy(slot, self.peer1, h - 1 + d).wait_recv()
            self.copy(slot, self.peer1, h - 1 + d).start()
            self.copy(slot, self.peer0, 2 * h - 1 + d).start()

    def third(self):
        h = self.high
        for d in range(h):
            slot = self.slot(d, 1 - self.b1, self.b0)
            self.copy(slot, self.peer0, 3 * h - 1 + d).wait_recv()
            self.copy(slot, self.peer0, 3 * h - 1 + d).start()

    def finish(self):
        h = self.high
        for b1 in (self.b1, 1 - self.b1):
            for d in range(h):
                slot = self.slot(d, b1, 1 - self.b0)
                self.copy(slot, self.peer0, 0).wait_recv()
        for k in range(4 * h - 1):
            self.copy(self.me, self.peer0, k).wait_send()


def head_column(offset_ref, heads, picked):
    rows = iota((heads * picked, 1), 0) // picked
    column = jnp.zeros((heads * picked, 1), jnp.int32)
    for h in range(heads):
        column = jnp.where(rows == h, offset_ref[h], column)
    return column


def kernel(
    n, heads, picked, stride,
    seg_ref, glob_ref, gain1_ref, gain_mlp_ref, gain2_ref, x_hbm,
    wq1_hbm, wk1_hbm, wv1_hbm, wo1_hbm, up_hbm, down_hbm, wq2_hbm, wk2_hbm, wv2_hbm, wo2_hbm,
    out_ref, back_ref,
    x_ref, wq1, wk1, wv1, wo1, up, down, wq2, wk2, wv2, wo2, wo_pad1, wo_pad2,
    xp, q, kv1, kv2, km, vp, moves, perm, mix, inner, sem, ssem1, rsem1, ssem2, rsem2,
):
    tokens, width = x_ref.shape
    size = width // heads
    half = LANES // 2
    chunk = heads * picked
    chunks = tokens // chunk
    keys = n * picked
    group = WINDOW // stride
    scale = size ** -0.5 * math.log2(math.e)

    pairs = [(wk1_hbm, wk1), (wv1_hbm, wv1), (wq1_hbm, wq1), (wo1_hbm, wo1), (up_hbm, up),
             (down_hbm, down), (wk2_hbm, wk2), (wv2_hbm, wv2), (wq2_hbm, wq2), (wo2_hbm, wo2)]
    loads = [pltpu.make_async_copy(a, b, sem.at[i]) for i, (a, b) in enumerate(pairs)]
    tokens_load = pltpu.make_async_copy(x_hbm, x_ref, sem.at[len(pairs)])
    tokens_load.start()
    loads[0].start()
    loads[1].start()

    first_gather = Gather(n, kv1, ssem1, rsem1)
    second_gather = Gather(n, kv2, ssem2, rsem2)
    barrier = pltpu.get_barrier_semaphore()
    peers = first_gather.peers()
    for peer in peers:
        pl.semaphore_signal(barrier, inc=1, device_id={"seq": peer}, device_id_type=MESH)

    def own_heads(hidden, weight):
        full = dot32(hidden, weight[...])
        column = iota((picked, width), 1)
        total = jnp.zeros((picked, width), F32)
        for h in range(heads):
            mine = (column >= h * size) & (column < h * size + size)
            total = jnp.where(mine, full[h * picked:(h + 1) * picked], total)
        return total.astype(BF16)

    rows = iota((chunk, 1), 0)
    pick = rows % picked
    target = pick * stride + head_column(seg_ref, heads, picked)
    onehot = (iota((chunk, tokens), 1) == target).astype(F32).astype(BF16)
    tokens_load.wait()
    hidden = norm_rows(dot32(onehot, x_ref[...]), gain1_ref[...][None, :])
    me = first_gather.me
    loads[0].wait()
    kv1[me, 0:picked, :] = own_heads(hidden, wk1)
    loads[1].wait()
    for load in loads[2:]:
        load.start()
    kv1[me, picked:2 * picked, :] = own_heads(hidden, wv1)
    pl.semaphore_wait(barrier, len(peers))
    first_gather.start()

    glob_col = head_column(glob_ref, heads, picked)
    lane = iota((16, WINDOW), 1)
    inside = lane % stride
    chosen = jnp.zeros((16, WINDOW), F32)
    for h in range(heads):
        chosen = jnp.where(inside == glob_ref[h], 1.0, chosen)
    a, b = iota((WINDOW, WINDOW), 0), iota((WINDOW, WINDOW), 1)
    same = a // stride == b // stride
    before = jnp.where(same & (a < b), 1.0, 0.0).astype(BF16)
    count = dot32(chosen.astype(BF16), before)
    total = dot32(chosen.astype(BF16), jnp.where(same, 1.0, 0.0).astype(BF16))
    rank = jnp.where(chosen > 0.5, count, total + inside.astype(F32) - count)
    rank_row = rank[0:1, :]
    table = jnp.where(same & (rank_row == (a % stride).astype(F32)), 1.0, 0.0)
    perm[...] = table.astype(BF16)
    back_ref[...] = table.T.astype(BF16)
    at_head = (iota((chunk, WINDOW), 1) == glob_col)
    head_rank = jnp.sum(jnp.where(at_head, rank_row, 0.0), axis=1, keepdims=True)
    spot = (pick * heads).astype(F32) + head_rank
    onehot_two = (iota((chunk, chunk), 1).astype(F32) == spot).astype(F32).astype(BF16)

    for g in range(tokens // WINDOW):
        moved = dot32(perm[...], x_ref[g * WINDOW:(g + 1) * WINDOW, :]).astype(BF16)
        for j in range(group):
            for c in range(chunks):
                at = c * chunk + (g * group + j) * heads
                xp[at:at + heads, :] = moved[j * stride + c * heads:j * stride + (c + 1) * heads]

    def window_of(h):
        return min(h * size // LANES * LANES, width - WINDOW)

    for h in range(heads):
        km[h] = jnp.zeros((WINDOW, keys), BF16)
        i = h % 2
        ones = iota((keys, LANES), 1) // half == i
        vp[h // 2, i * keys:(i + 1) * keys, LANES:] = jnp.where(ones, 1.0, 0.0).astype(BF16)
        source = iota((WINDOW, LANES), 0) - (h * size - window_of(h))
        goal = iota((WINDOW, LANES), 1) - i * half
        moves[h] = jnp.where((source == goal) & (goal >= 0) & (goal < size), 1.0, 0.0).astype(BF16)
    for source, padded, load in ((wo1, wo_pad1, loads[3]), (wo2, wo_pad2, None)):
        if load is None:
            continue
        load.wait()
        for h in range(heads):
            padded[h * half:h * half + size, :] = source[h * size:(h + 1) * size, :]
            padded[h * half + size:(h + 1) * half, :] = jnp.zeros((half - size, width), BF16)

    first_gather.second()

    loads[2].wait()

    large = 2 * chunk

    def query_chunk(c, carry):
        at = pl.ds(pl.multiple_of(c * large, large), large)
        hidden = norm_rows(xp[at, :].astype(F32), gain1_ref[...][None, :])
        q[at, :] = dot32(hidden, wq1[...]).astype(BF16)
        return carry

    lax.fori_loop(0, tokens // large, query_chunk, 0)
    first_gather.third()
    first_gather.finish()

    def set_keys(kv):
        key = kv[:, 0:picked, :].reshape(keys, width)
        value = kv[:, picked:2 * picked, :].reshape(keys, width)
        turned = key.astype(F32).T.astype(BF16)
        for h in range(heads):
            begin = h * size - window_of(h)
            km[h, begin:begin + size, :] = turned[h * size:(h + 1) * size, :]
            i = h % 2
            moved = dot32(value[:, window_of(h):window_of(h) + WINDOW], moves[h])
            vp[h // 2, i * keys:(i + 1) * keys, 0:LANES] = moved.astype(BF16)

    def attend(at, count):
        for pair in range(heads // 2):
            parts = []
            for h in (2 * pair, 2 * pair + 1):
                start = window_of(h)
                scores = dot32(q[at, start:start + WINDOW], km[h])
                top = jnp.max(scores, axis=-1, keepdims=True)
                parts.append(jnp.exp2((scores - top) * scale).astype(BF16))
            both = dot32(jnp.concatenate(parts, axis=1), vp[pair])
            mixed = both[:, :LANES] / both[:, LANES:]
            mix[0:count, pair * LANES:(pair + 1) * LANES] = mixed.astype(BF16)

    set_keys(kv1)

    def first_layer(begin, count, after_attention, after_up):
        at = slice(begin, begin + count)
        attend(at, count)
        first = xp[at, :].astype(F32) + dot32(mix[0:count, :], wo_pad1[...])
        xp[at, :] = first.astype(BF16)
        after_attention()
        normed = norm_rows(xp[at, :].astype(F32), gain_mlp_ref[...][None, :])
        for start in range(0, up.shape[1], width):
            part = dot32(normed, up[:, start:start + width])
            inner[0:count, start:start + width] = gelu(part).astype(BF16)
        after_up()
        second = xp[at, :].astype(F32) + dot32(inner[0:count, :], down[...])
        xp[at, :] = second.astype(BF16)
        hidden_two = norm_rows(xp[at, :].astype(F32), gain2_ref[...][None, :])
        q[at, :] = dot32(hidden_two, wq2[...]).astype(BF16)
        return hidden_two

    def wait_for(*which):
        for i in which:
            loads[i].wait()

    hidden_two = first_layer(0, chunk, lambda: wait_for(4, 5), lambda: wait_for(6, 7, 8))
    picked_rows = dot32(onehot_two, hidden_two).astype(BF16)
    kv2[me, 0:picked, :] = own_heads(picked_rows, wk2)
    kv2[me, picked:2 * picked, :] = own_heads(picked_rows, wv2)
    second_gather.start()
    first_layer(chunk, tokens - chunk, second_gather.second, second_gather.third)

    loads[9].wait()
    for h in range(heads):
        wo_pad2[h * half:h * half + size, :] = wo2[h * size:(h + 1) * size, :]
        wo_pad2[h * half + size:(h + 1) * half, :] = jnp.zeros((half - size, width), BF16)
    second_gather.finish()
    set_keys(kv2)

    def last_chunk(c, carry):
        at = pl.ds(pl.multiple_of(c * large, large), large)
        attend(at, large)
        done = xp[at, :].astype(F32) + dot32(mix[0:large, :], wo_pad2[...])
        done = done.astype(BF16)
        for i in range(large // chunk):
            for j in range(picked):
                row = pl.multiple_of(j * stride + (c * (large // chunk) + i) * heads, heads)
                block = i * chunk + j * heads
                out_ref[pl.ds(row, heads), :] = done[block:block + heads]
        return carry

    lax.fori_loop(0, tokens // large, last_chunk, 0)


def reorder_kernel(back_ref, x_ref, out_ref):
    out_ref[...] = dot32(back_ref[...], x_ref[...]).astype(BF16)


def whole_body(
    tokens, attn_gain, query_first, key_first, segment_value, output_first, mlp_gain, up_weight,
    down_weight, second_gain, query_second, key_second, value_second, output_second,
    segment_offset, global_offset,
):
    n = lax.axis_size("seq")
    heads = segment_offset.shape[0]
    picked = KEYS // n
    count, width = tokens.shape
    stride = count // picked
    units = up_weight.shape[1]
    chunk = heads * picked
    any_space = pl.BlockSpec(memory_space=pl.ANY)
    vmem = pl.BlockSpec(memory_space=pltpu.VMEM)
    smem = pl.BlockSpec(memory_space=pltpu.SMEM)
    square = pltpu.VMEM((width, width), BF16)
    padded = pltpu.VMEM((heads * LANES // 2, width), BF16)
    done, back = pl.pallas_call(
        functools.partial(kernel, n, heads, picked, stride),
        out_shape=(
            jax.ShapeDtypeStruct(tokens.shape, BF16),
            jax.ShapeDtypeStruct((WINDOW, WINDOW), BF16),
        ),
        in_specs=[smem, smem, vmem, vmem, vmem] + [any_space] * 11,
        out_specs=(vmem, vmem),
        scratch_shapes=[
            pltpu.VMEM((count, width), BF16),
            square, square, square, square,
            pltpu.VMEM((width, units), BF16), pltpu.VMEM((units, width), BF16),
            square, square, square, square, padded, padded,
            pltpu.VMEM((count, width), BF16),
            pltpu.VMEM((count, width), BF16),
            pltpu.VMEM((n, 2 * picked, width), BF16),
            pltpu.VMEM((n, 2 * picked, width), BF16),
            pltpu.VMEM((heads, WINDOW, KEYS), BF16),
            pltpu.VMEM((heads // 2, 2 * KEYS, 2 * LANES), BF16),
            pltpu.VMEM((heads, WINDOW, LANES), BF16),
            pltpu.VMEM((WINDOW, WINDOW), BF16),
            pltpu.VMEM((count - chunk, heads * LANES // 2), BF16),
            pltpu.VMEM((count - chunk, units), BF16),
            pltpu.SemaphoreType.DMA((11,)),
            pltpu.SemaphoreType.DMA((n,)), pltpu.SemaphoreType.DMA((n,)),
            pltpu.SemaphoreType.DMA((n,)), pltpu.SemaphoreType.DMA((n,)),
        ],
        compiler_params=pltpu.CompilerParams(
            collective_id=0, has_side_effects=True, vmem_limit_bytes=VMEM_BYTES
        ),
        name="encoder",
    )(
        segment_offset, global_offset, attn_gain, mlp_gain, second_gain, tokens,
        query_first, key_first, segment_value, output_first, up_weight, down_weight,
        query_second, key_second, value_second, output_second,
    )
    rows = pl.BlockSpec((WINDOW, width), lambda i: (i, 0))
    return pl.pallas_call(
        reorder_kernel,
        grid=(count // WINDOW,),
        out_shape=jax.ShapeDtypeStruct(tokens.shape, BF16),
        in_specs=[pl.BlockSpec((WINDOW, WINDOW), lambda i: (0, 0)), rows],
        out_specs=rows,
        compiler_params=pltpu.CompilerParams(vmem_limit_bytes=VMEM_BYTES),
        name="reorder",
    )(back, done)


def fits(mesh):
    n = mesh.shape["seq"]
    return mesh.shape["mp"] == 1 and n == SEG_MAX


def choose(mesh):
    return whole_body if fits(mesh) else body


def solution(mesh):
    placed = (
        P(("slides", "seq", "mp"), None),
        P(),
        P(None, "mp"),
        P(None, "mp"),
        P(None, "mp"),
        P("mp", None),
        P(),
        P(None, "mp"),
        P("mp", None),
        P(),
        P(None, "mp"),
        P(None, "mp"),
        P(None, "mp"),
        P("mp", None),
        P("mp"),
        P("mp"),
    )
    return jax.shard_map(
        choose(mesh),
        mesh=mesh,
        in_specs=placed,
        out_specs=P(("slides", "seq", "mp"), None),
        check_vma=False,
    )
```

```python
import functools
import math

import jax
import jax.numpy as jnp
from jax import lax
from jax.experimental import pallas as pl
from jax.experimental.pallas import tpu as pltpu
from jax.sharding import PartitionSpec as P

KEYS = 256
SEG_MAX = 16


def swapped(x, axis, apart):
    return lax.ppermute(x, axis, [(i, i ^ 1 << apart) for i in range(lax.axis_size(axis))])


def norm_rows(values, gain):
    center = values - jnp.mean(values, axis=-1, keepdims=True)
    spread = jnp.mean(center * center, axis=-1, keepdims=True)
    return (center * lax.rsqrt(spread + 1e-05) * gain).astype(jnp.bfloat16)


def pick_keys(hidden, offsets, stride, key_weight, value_weight):
    token_count, width = hidden.shape
    head_count = offsets.shape[0]
    head_size = key_weight.shape[1] // head_count
    grouped_rows = hidden.reshape(token_count // stride, stride, width)
    dilation_selector = (
        lax.broadcasted_iota(jnp.int32, (stride, head_count), 0) == offsets[None, :]
    ).astype(jnp.bfloat16)
    chosen = jnp.einsum(
        "nof,oj->njf", grouped_rows, dilation_selector, preferred_element_type=jnp.float32
    ).astype(jnp.bfloat16)
    key_heads = jnp.einsum(
        "xkr,rkf->xkf",
        chosen,
        key_weight.reshape(width, head_count, head_size),
        preferred_element_type=jnp.float32,
    ).astype(jnp.bfloat16)
    value_heads = jnp.einsum(
        "xkr,rkf->xkf",
        chosen,
        value_weight.reshape(width, head_count, head_size),
        preferred_element_type=jnp.float32,
    ).astype(jnp.bfloat16)
    picked = token_count // stride
    return jnp.stack(
        [
            key_heads.reshape(picked, head_count * head_size),
            value_heads.reshape(picked, head_count * head_size),
        ]
    )


def attend_local(query, keyval, head_count):
    token_count, width = query.shape
    head_size = width // head_count
    query_heads = query.reshape(token_count, head_count, head_size)
    key_heads = keyval[0].reshape(-1, head_count, head_size)
    value_heads = keyval[1].reshape(-1, head_count, head_size)
    scores = jnp.einsum(
        "thd,khd->htk", query_heads, key_heads, preferred_element_type=jnp.float32
    ) * head_size ** (-0.5)
    highest = jnp.max(scores, axis=-1, keepdims=True)
    weights = jnp.exp(scores - highest)
    weights = (weights / jnp.sum(weights, axis=-1, keepdims=True)).astype(jnp.bfloat16)
    mixed = jnp.einsum(
        "htk,khd->thd", weights, value_heads, preferred_element_type=jnp.float32
    ).astype(jnp.bfloat16)
    return mixed.reshape(token_count, width)


def merge_branch_pair(mine, other, level, token_position):
    lower = token_position >> level & 1 == 0
    return jnp.where(
        lower, jnp.concatenate((mine, other), axis=1), jnp.concatenate((other, mine), axis=1)
    )


def spread_segment(keyval, seg_span, token_position):
    for level in range(seg_span.bit_length() - 1):
        partner = swapped(keyval, "seq", level)
        keyval = merge_branch_pair(keyval, partner, level, token_position)
    return keyval


def spread_global(keyval_two):
    keyval_two = lax.all_gather(keyval_two, "seq", axis=1, tiled=True)
    return keyval_two


def combine(partial_value, residual_full, need_full):
    row_count = residual_full.shape[0] // lax.axis_size("mp")
    row_start = lax.axis_index("mp") * row_count
    share = lax.psum_scatter(partial_value, "mp", scatter_dimension=0, tiled=True)
    own_rows = lax.dynamic_slice_in_dim(residual_full, row_start, row_count, 0)
    own_rows = (own_rows.astype(jnp.float32) + share).astype(jnp.bfloat16)
    full_rows = lax.all_gather(own_rows, "mp", axis=0, tiled=True) if need_full else own_rows
    return (own_rows, full_rows)


def body(
    tokens,
    attn_gain,
    query_first,
    key_first,
    segment_value,
    output_first,
    mlp_gain,
    up_weight,
    down_weight,
    second_gain,
    query_second,
    key_second,
    value_second,
    output_second,
    segment_offset,
    global_offset,
):
    seq_count = lax.axis_size("seq")
    token_position = lax.axis_index("seq")
    seg_span = min(SEG_MAX, seq_count)
    head_count = segment_offset.shape[0]
    full_rows = lax.all_gather(tokens, "mp", axis=0, tiled=True)
    token_count = full_rows.shape[0]
    hidden = norm_rows(full_rows.astype(jnp.float32), attn_gain)
    query = jnp.dot(hidden, query_first, preferred_element_type=jnp.float32).astype(jnp.bfloat16)
    seg_stride = token_count // (KEYS // seg_span)
    keyval = pick_keys(hidden, segment_offset, seg_stride, key_first, segment_value)
    keyval = spread_segment(keyval, seg_span, token_position)
    mixed = attend_local(query, keyval, head_count)
    partial_value = jnp.dot(mixed, output_first, preferred_element_type=jnp.float32)
    own_rows, first_rows = combine(partial_value, full_rows, True)
    normed = norm_rows(first_rows.astype(jnp.float32), mlp_gain)
    inner = jax.nn.gelu(
        jnp.dot(normed, up_weight, preferred_element_type=jnp.float32), approximate=True
    ).astype(jnp.bfloat16)
    partial_value = jnp.dot(inner, down_weight, preferred_element_type=jnp.float32)
    own_rows, second_rows = combine(partial_value, first_rows, True)
    hidden_two = norm_rows(second_rows.astype(jnp.float32), second_gain)
    query_two = jnp.dot(hidden_two, query_second, preferred_element_type=jnp.float32).astype(
        jnp.bfloat16
    )
    glob_stride = token_count // (KEYS // seq_count)
    keyval_two = pick_keys(hidden_two, global_offset, glob_stride, key_second, value_second)
    keyval_two = spread_global(keyval_two)
    mixed_two = attend_local(query_two, keyval_two, head_count)
    partial_value = jnp.dot(mixed_two, output_second, preferred_element_type=jnp.float32)
    own_rows, unused_rows = combine(partial_value, second_rows, False)
    return own_rows


MESH = pl.DeviceIdType.MESH
F32 = jnp.float32
BF16 = jnp.bfloat16
WINDOW = 256
LANES = 128
VMEM_BYTES = 62 << 20


def iota(shape, axis):
    return lax.broadcasted_iota(jnp.int32, shape, axis)


def dot32(a, b):
    return jnp.dot(a, b, preferred_element_type=F32)


def gelu(x):
    return 0.5 * x * (1.0 + jnp.tanh(math.sqrt(2.0 / math.pi) * (x + 0.044715 * (x * x * x))))


class Gather:
    def __init__(self, n, buf, ssem, rsem):
        me = lax.axis_index("seq")
        self.me, self.n, self.high = me, n, n // 4
        self.buf, self.ssem, self.rsem = buf, ssem, rsem
        self.b0, self.b1, self.hi = me % 2, (me // 2) % 2, me // 4
        self.peer1 = self.hi * 4 + (1 - self.b1) * 2 + self.b0
        self.peer0 = self.hi * 4 + self.b1 * 2 + (1 - self.b0)

    def slot(self, d, b1, b0):
        return ((self.hi + self.high - d) % self.high) * 4 + b1 * 2 + b0

    def copy(self, slot, peer, k):
        return pltpu.make_async_remote_copy(
            src_ref=self.buf.at[slot],
            dst_ref=self.buf.at[slot],
            send_sem=self.ssem.at[k],
            recv_sem=self.rsem.at[slot],
            device_id={"seq": peer},
            device_id_type=MESH,
        )

    def peers(self):
        out = [((self.hi + d) % self.high) * 4 + self.b1 * 2 + self.b0 for d in range(1, self.high)]
        return out + [self.peer1, self.peer0]

    def start(self):
        h = self.high
        for d in range(1, h):
            peer = ((self.hi + d) % h) * 4 + self.b1 * 2 + self.b0
            self.copy(self.me, peer, d - 1).start()
        self.copy(self.me, self.peer1, h - 1).start()
        self.copy(self.me, self.peer0, 2 * h - 1).start()

    def second(self):
        h = self.high
        for d in range(1, h):
            slot = self.slot(d, self.b1, self.b0)
            self.copy(slot, self.peer1, h - 1 + d).wait_recv()
            self.copy(slot, self.peer1, h - 1 + d).start()
            self.copy(slot, self.peer0, 2 * h - 1 + d).start()

    def third(self):
        h = self.high
        for d in range(h):
            slot = self.slot(d, 1 - self.b1, self.b0)
            self.copy(slot, self.peer0, 3 * h - 1 + d).wait_recv()
            self.copy(slot, self.peer0, 3 * h - 1 + d).start()

    def finish(self):
        h = self.high
        for b1 in (self.b1, 1 - self.b1):
            for d in range(h):
                slot = self.slot(d, b1, 1 - self.b0)
                self.copy(slot, self.peer0, 0).wait_recv()
        for k in range(4 * h - 1):
            self.copy(self.me, self.peer0, k).wait_send()


def head_column(offset_ref, heads, picked):
    rows = iota((heads * picked, 1), 0) // picked
    column = jnp.zeros((heads * picked, 1), jnp.int32)
    for h in range(heads):
        column = jnp.where(rows == h, offset_ref[h], column)
    return column


def kernel(
    n, heads, picked, stride,
    seg_ref, glob_ref, gain1_ref, gain_mlp_ref, gain2_ref, x_hbm,
    wq1_hbm, wk1_hbm, wv1_hbm, wo1_hbm, up_hbm, down_hbm, wq2_hbm, wk2_hbm, wv2_hbm, wo2_hbm,
    out_ref,
    x_ref, wq1, wk1, wv1, wo1, up, down, wq2, wk2, wv2, wo2, wo_pad1, wo_pad2,
    xp, q, kv1, kv2, km, vp, moves, perm, perm_back, mix, inner, sem, ssem1, rsem1, ssem2, rsem2,
):
    tokens, width = x_ref.shape
    size = width // heads
    half = LANES // 2
    chunk = heads * picked
    chunks = tokens // chunk
    keys = n * picked
    group = WINDOW // stride
    scale = size ** -0.5 * math.log2(math.e)

    pairs = [(wk1_hbm, wk1), (wv1_hbm, wv1), (wq1_hbm, wq1), (wo1_hbm, wo1), (up_hbm, up),
             (down_hbm, down), (wk2_hbm, wk2), (wv2_hbm, wv2), (wq2_hbm, wq2), (wo2_hbm, wo2)]
    loads = [pltpu.make_async_copy(a, b, sem.at[i]) for i, (a, b) in enumerate(pairs)]
    tokens_load = pltpu.make_async_copy(x_hbm, x_ref, sem.at[len(pairs)])
    tokens_load.start()
    loads[0].start()
    loads[1].start()

    first_gather = Gather(n, kv1, ssem1, rsem1)
    second_gather = Gather(n, kv2, ssem2, rsem2)
    barrier = pltpu.get_barrier_semaphore()
    peers = first_gather.peers()
    for peer in peers:
        pl.semaphore_signal(barrier, inc=1, device_id={"seq": peer}, device_id_type=MESH)

    def own_heads(hidden, weight):
        full = dot32(hidden, weight[...])
        column = iota((picked, width), 1)
        total = jnp.zeros((picked, width), F32)
        for h in range(heads):
            mine = (column >= h * size) & (column < h * size + size)
            total = jnp.where(mine, full[h * picked:(h + 1) * picked], total)
        return total.astype(BF16)

    rows = iota((chunk, 1), 0)
    pick = rows % picked
    target = pick * stride + head_column(seg_ref, heads, picked)
    onehot = (iota((chunk, tokens), 1) == target).astype(F32).astype(BF16)
    tokens_load.wait()
    hidden = norm_rows(dot32(onehot, x_ref[...]), gain1_ref[...][None, :])
    me = first_gather.me
    loads[0].wait()
    kv1[me, 0:picked, :] = own_heads(hidden, wk1)
    loads[1].wait()
    loads[2].start()
    kv1[me, picked:2 * picked, :] = own_heads(hidden, wv1)
    pl.semaphore_wait(barrier, len(peers))
    first_gather.start()

    glob_col = head_column(glob_ref, heads, picked)
    lane = iota((16, WINDOW), 1)
    inside = lane % stride
    chosen = jnp.zeros((16, WINDOW), F32)
    for h in range(heads):
        chosen = jnp.where(inside == glob_ref[h], 1.0, chosen)
    a, b = iota((WINDOW, WINDOW), 0), iota((WINDOW, WINDOW), 1)
    same = a // stride == b // stride
    before = jnp.where(same & (a < b), 1.0, 0.0).astype(BF16)
    count = dot32(chosen.astype(BF16), before)
    total = dot32(chosen.astype(BF16), jnp.where(same, 1.0, 0.0).astype(BF16))
    rank = jnp.where(chosen > 0.5, count, total + inside.astype(F32) - count)
    rank_row = rank[0:1, :]
    table = jnp.where(same & (rank_row == (a % stride).astype(F32)), 1.0, 0.0)
    perm[...] = table.astype(BF16)
    perm_back[...] = table.T.astype(BF16)
    at_head = (iota((chunk, WINDOW), 1) == glob_col)
    head_rank = jnp.sum(jnp.where(at_head, rank_row, 0.0), axis=1, keepdims=True)
    spot = (pick * heads).astype(F32) + head_rank
    onehot_two = (iota((chunk, chunk), 1).astype(F32) == spot).astype(F32).astype(BF16)

    for g in range(tokens // WINDOW):
        moved = dot32(perm[...], x_ref[g * WINDOW:(g + 1) * WINDOW, :]).astype(BF16)
        for j in range(group):
            for c in range(chunks):
                at = c * chunk + (g * group + j) * heads
                xp[at:at + heads, :] = moved[j * stride + c * heads:j * stride + (c + 1) * heads]

    def window_of(h):
        return min(h * size // LANES * LANES, width - WINDOW)

    loads[2].wait()
    for load in loads[3:]:
        load.start()

    large = 2 * chunk

    def query_chunk(c, carry):
        at = pl.ds(pl.multiple_of(c * large, large), large)
        hidden = norm_rows(xp[at, :].astype(F32), gain1_ref[...][None, :])
        q[at, :] = dot32(hidden, wq1[...]).astype(BF16)
        return carry

    lax.fori_loop(0, tokens // large, query_chunk, 0)
    first_gather.second()
    for h in range(heads):
        km[h] = jnp.zeros((WINDOW, keys), BF16)
        i = h % 2
        ones = iota((keys, LANES), 1) // half == i
        vp[h // 2, i * keys:(i + 1) * keys, LANES:] = jnp.where(ones, 1.0, 0.0).astype(BF16)
        source = iota((WINDOW, LANES), 0) - (h * size - window_of(h))
        goal = iota((WINDOW, LANES), 1) - i * half
        moves[h] = jnp.where((source == goal) & (goal >= 0) & (goal < size), 1.0, 0.0).astype(BF16)
    first_gather.third()
    first_gather.finish()

    def set_keys(kv):
        key = kv[:, 0:picked, :].reshape(keys, width)
        value = kv[:, picked:2 * picked, :].reshape(keys, width)
        turned = key.astype(F32).T.astype(BF16)
        for h in range(heads):
            begin = h * size - window_of(h)
            km[h, begin:begin + size, :] = turned[h * size:(h + 1) * size, :]
            i = h % 2
            moved = dot32(value[:, window_of(h):window_of(h) + WINDOW], moves[h])
            vp[h // 2, i * keys:(i + 1) * keys, 0:LANES] = moved.astype(BF16)

    def attend(at, count):
        for pair in range(heads // 2):
            parts = []
            for h in (2 * pair, 2 * pair + 1):
                start = window_of(h)
                scores = dot32(q[at, start:start + WINDOW], km[h])
                top = jnp.max(scores, axis=-1, keepdims=True)
                parts.append(jnp.exp2((scores - top) * scale).astype(BF16))
            both = dot32(jnp.concatenate(parts, axis=1), vp[pair])
            mixed = both[:, :LANES] / both[:, LANES:]
            mix[0:count, pair * LANES:(pair + 1) * LANES] = mixed.astype(BF16)

    def pad_rows(source, padded):
        for h in range(heads):
            padded[h * half:h * half + size, :] = source[h * size:(h + 1) * size, :]
            padded[h * half + size:(h + 1) * half, :] = jnp.zeros((half - size, width), BF16)

    set_keys(kv1)
    loads[3].wait()
    pad_rows(wo1, wo_pad1)

    def first_layer(begin, count, after_attention, after_up):
        at = slice(begin, begin + count)
        attend(at, count)
        first = xp[at, :].astype(F32) + dot32(mix[0:count, :], wo_pad1[...])
        xp[at, :] = first.astype(BF16)
        after_attention()
        normed = norm_rows(xp[at, :].astype(F32), gain_mlp_ref[...][None, :])
        for start in range(0, up.shape[1], width):
            part = dot32(normed, up[:, start:start + width])
            inner[0:count, start:start + width] = gelu(part).astype(BF16)
        after_up()
        second = xp[at, :].astype(F32) + dot32(inner[0:count, :], down[...])
        xp[at, :] = second.astype(BF16)
        hidden_two = norm_rows(xp[at, :].astype(F32), gain2_ref[...][None, :])
        q[at, :] = dot32(hidden_two, wq2[...]).astype(BF16)
        return hidden_two

    def wait_for(*which):
        for i in which:
            loads[i].wait()

    hidden_two = first_layer(0, chunk, lambda: wait_for(4, 5), lambda: wait_for(6, 7, 8))
    picked_rows = dot32(onehot_two, hidden_two).astype(BF16)
    kv2[me, 0:picked, :] = own_heads(picked_rows, wk2)
    kv2[me, picked:2 * picked, :] = own_heads(picked_rows, wv2)
    second_gather.start()
    first_layer(chunk, tokens - chunk, second_gather.second, second_gather.third)

    loads[9].wait()
    pad_rows(wo2, wo_pad2)
    second_gather.finish()
    set_keys(kv2)

    def last_chunk(c, carry):
        at = pl.ds(pl.multiple_of(c * large, large), large)
        attend(at, large)
        done = xp[at, :].astype(F32) + dot32(mix[0:large, :], wo_pad2[...])
        xp[at, :] = done.astype(BF16)
        return carry

    lax.fori_loop(0, tokens // large, last_chunk, 0)
    for g in range(tokens // WINDOW):
        blocks = []
        for j in range(group):
            for c in range(chunks):
                begin = c * chunk + (g * group + j) * heads
                blocks.append(xp[begin:begin + heads, :])
        moved = dot32(perm_back[...], jnp.concatenate(blocks, axis=0))
        out_ref[g * WINDOW:(g + 1) * WINDOW, :] = moved.astype(BF16)


def whole_body(
    tokens, attn_gain, query_first, key_first, segment_value, output_first, mlp_gain, up_weight,
    down_weight, second_gain, query_second, key_second, value_second, output_second,
    segment_offset, global_offset,
):
    n = lax.axis_size("seq")
    heads = segment_offset.shape[0]
    picked = KEYS // n
    count, width = tokens.shape
    stride = count // picked
    units = up_weight.shape[1]
    chunk = heads * picked
    any_space = pl.BlockSpec(memory_space=pl.ANY)
    vmem = pl.BlockSpec(memory_space=pltpu.VMEM)
    smem = pl.BlockSpec(memory_space=pltpu.SMEM)
    square = pltpu.VMEM((width, width), BF16)
    padded = pltpu.VMEM((heads * LANES // 2, width), BF16)
    return pl.pallas_call(
        functools.partial(kernel, n, heads, picked, stride),
        out_shape=jax.ShapeDtypeStruct(tokens.shape, BF16),
        in_specs=[smem, smem, vmem, vmem, vmem] + [any_space] * 11,
        out_specs=vmem,
        scratch_shapes=[
            pltpu.VMEM((count, width), BF16),
            square, square, square, square,
            pltpu.VMEM((width, units), BF16), pltpu.VMEM((units, width), BF16),
            square, square, square, square, padded, padded,
            pltpu.VMEM((count, width), BF16),
            pltpu.VMEM((count, width), BF16),
            pltpu.VMEM((n, 2 * picked, width), BF16),
            pltpu.VMEM((n, 2 * picked, width), BF16),
            pltpu.VMEM((heads, WINDOW, KEYS), BF16),
            pltpu.VMEM((heads // 2, 2 * KEYS, 2 * LANES), BF16),
            pltpu.VMEM((heads, WINDOW, LANES), BF16),
            pltpu.VMEM((WINDOW, WINDOW), BF16),
            pltpu.VMEM((WINDOW, WINDOW), BF16),
            pltpu.VMEM((count - chunk, heads * LANES // 2), BF16),
            pltpu.VMEM((count - chunk, units), BF16),
            pltpu.SemaphoreType.DMA((11,)),
            pltpu.SemaphoreType.DMA((n,)), pltpu.SemaphoreType.DMA((n,)),
            pltpu.SemaphoreType.DMA((n,)), pltpu.SemaphoreType.DMA((n,)),
        ],
        compiler_params=pltpu.CompilerParams(
            collective_id=0, has_side_effects=True, vmem_limit_bytes=VMEM_BYTES
        ),
        name="encoder",
    )(
        segment_offset, global_offset, attn_gain, mlp_gain, second_gain, tokens,
        query_first, key_first, segment_value, output_first, up_weight, down_weight,
        query_second, key_second, value_second, output_second,
    )


def fits(mesh):
    n = mesh.shape["seq"]
    return mesh.shape["mp"] == 1 and n == SEG_MAX


def choose(mesh):
    return whole_body if fits(mesh) else body


def solution(mesh):
    placed = (
        P(("slides", "seq", "mp"), None),
        P(),
        P(None, "mp"),
        P(None, "mp"),
        P(None, "mp"),
        P("mp", None),
        P(),
        P(None, "mp"),
        P("mp", None),
        P(),
        P(None, "mp"),
        P(None, "mp"),
        P(None, "mp"),
        P("mp", None),
        P("mp"),
        P("mp"),
    )
    return jax.shard_map(
        choose(mesh),
        mesh=mesh,
        in_specs=placed,
        out_specs=P(("slides", "seq", "mp"), None),
        check_vma=False,
    )
```
